768 devices in a mesh: blk: 24 (over x, z_hi, core), sub: 32 (over z_lo, y).
Axes of the slice: x: 4, y: 8, z: 12 (z_hi: 3, z_lo: 4; z = z_hi * 4 + z_lo), core: 2. Of those that a mesh axis runs over, the one named last changes fastest.
Arguments:
- images: bfloat16 [393216, 768], P(('blk', 'sub')), may hold values from -6 to 6
- texts: bfloat16 [393216, 768], P(('blk', 'sub')), may hold values from -6 to 6
- logit_scale: float32 [1], replicated, may hold values from 2 to 10
- logit_bias: float32 [1], replicated, may hold values from -4 to -1
Outputs:
- grad_images: float32 [393216, 768], P(('blk', 'sub'))
- grad_texts: float32 [393216, 768], P(('blk', 'sub'))
The draws below stay inside these ranges and needn't reach their ends.
All inputs are finite; a program needn't handle non-finite values.
Results may differ from the reference program's by a relative error of at most 0.004.
Values may be sent and summed in bfloat16 or wider, within the bound.
A program may use at most 32 MiB of HBM per device.

```python
import math
import jax
import jax.numpy as jnp
from jax import lax

EMBED = 768
B_DEV = 512
N_ROWS = 393216
N_BLK = 24
N_SUB = 32


def block_levels(rng, extent, pieces, least, high):
    loudness, own = 1.0, jax.random.fold_in(rng, 6)
    for axis_at, shards_of in pieces:
        heights = jnp.exp(jax.random.uniform(jax.random.fold_in(own, axis_at), (shards_of,), jnp.float32, least / len(pieces), high / len(pieces)))
        loudness = loudness * jnp.repeat(heights, extent[axis_at] // shards_of).reshape([-1 if axis == axis_at else 1 for axis in range(len(extent))])
    return loudness


def scatter_about(stream_key, shape, scale, reach, split=(), held_as=jnp.bfloat16):
    values = jax.random.normal(stream_key, shape, jnp.float32) * scale
    if len(split) > 0:
        values = block_levels(stream_key, shape, split, -0.22, 0.18) * values
    return jnp.clip(values, min=-reach, max=reach).astype(held_as)


def setup_inputs(seed: int = 0) -> dict:
    key_list = jax.random.split(jax.random.key(seed), 5)
    return {
        "images": scatter_about(key_list[0], (N_ROWS, EMBED), 1.0, 6.0, ((0, 768),)),
        "texts": scatter_about(key_list[1], (N_ROWS, EMBED), 1.0, 6.0, ((0, 768),)),
        "logit_scale": jnp.clip(jnp.exp(jax.random.uniform(key_list[2], (1,), jnp.float32, math.log(2.0), math.log(10.0))), 2.0, 10.0),
        "logit_bias": jnp.clip(jax.random.uniform(key_list[3], (1,), jnp.float32, -4.0, -1.0), -4.0, -1.0),
    }


def unit_rows(values_in):
    values = values_in.astype(jnp.float32)
    recip = lax.rsqrt(lax.optimization_barrier(jnp.sum(values * values, axis=-1, keepdims=True)) + 1e-06)
    return (values * recip, recip)

def tile_weights(left, right, scale, offset):
    logits = scale * jnp.dot(left, right.T, preferred_element_type=jnp.float32) + offset
    return jax.nn.sigmoid(logits)

def contract_rows(weights, rows):
    return lax.dot_general(weights, rows, (((0,), (0,)), ((), ())), preferred_element_type=jnp.float32)

def back_norm(unit, recip, grad):
    return (grad - unit * lax.optimization_barrier(jnp.sum(unit * grad, axis=-1, keepdims=True))) * recip

def reference(images, texts, logit_scale, logit_bias):
    count = N_BLK * N_SUB
    unit_img, recip_img = unit_rows(images)
    unit_txt, recip_txt = unit_rows(texts)
    img_low = unit_img.astype(jnp.bfloat16).reshape(count, B_DEV, EMBED)
    txt_low = unit_txt.astype(jnp.bfloat16).reshape(count, B_DEV, EMBED)
    scale = logit_scale[0]
    offset = logit_bias[0]
    diagonal_one = jnp.eye(B_DEV, dtype=jnp.float32)

    def per_block(block_set):
        img_own, img_prev, img_next, txt_own, txt_prev, txt_next = block_set
        weight_own = (tile_weights(img_own, txt_own, scale, offset) - diagonal_one).astype(jnp.bfloat16)
        weight_prev = tile_weights(img_own, txt_prev, scale, offset).astype(jnp.bfloat16)
        weight_next = tile_weights(img_own, txt_next, scale, offset).astype(jnp.bfloat16)
        from_prev = tile_weights(img_prev, txt_own, scale, offset).astype(jnp.bfloat16)
        from_next = tile_weights(img_next, txt_own, scale, offset).astype(jnp.bfloat16)
        grad_img = scale * (jnp.dot(weight_own, txt_own, preferred_element_type=jnp.float32) + jnp.dot(weight_prev, txt_prev, preferred_element_type=jnp.float32) + jnp.dot(weight_next, txt_next, preferred_element_type=jnp.float32))
        grad_txt = scale * (contract_rows(weight_own, img_own) + contract_rows(from_prev, img_prev) + contract_rows(from_next, img_next))
        return (grad_img, grad_txt)
    grad_img, grad_txt = lax.map(per_block, (img_low, jnp.roll(img_low, 1, 0), jnp.roll(img_low, -1, 0), txt_low, jnp.roll(txt_low, 1, 0), jnp.roll(txt_low, -1, 0)))
    grad_img = grad_img.reshape(-1, EMBED)
    grad_txt = grad_txt.reshape(-1, EMBED)
    return (back_norm(unit_img, recip_img, grad_img), back_norm(unit_txt, recip_txt, grad_txt))
```

```python
import functools

import jax
import jax.numpy as jnp
from jax import lax
from jax.experimental import pallas as pl
from jax.experimental.pallas import tpu as pltpu
from jax.sharding import PartitionSpec as P

MESH = pl.DeviceIdType.MESH
RING = 8
ROWS = 64
BLOCK = 256
PART = 128


def unit_rows(raw):
    values = raw.astype(jnp.float32)
    recip = lax.rsqrt(jnp.sum(values * values, axis=-1, keepdims=True) + 1e-06)
    return values * recip, recip


def pair_weights(own, some, scale, bias):
    dots = lax.dot_general(own, some, (((1,), (1,)), ((), ())), preferred_element_type=jnp.float32)
    return jax.nn.sigmoid(scale * dots + bias)


def weighted(weights, some):
    return jnp.dot(weights.astype(jnp.bfloat16), some, preferred_element_type=jnp.float32)


def back_norm(raw, recip, grad):
    unit = raw.astype(jnp.float32) * recip
    return (grad - unit * jnp.sum(unit * grad, axis=-1, keepdims=True)) * recip


def exchange(n_blk, n_sub, scale_ref, bias_ref, img, txt, total, raw, low, recips, unit, scalars,
             arrived, load_sem, send_sem, recv_sem, ready_sem):
    count = n_blk * n_sub
    rows = img.shape[0]
    steps = rows // ROWS
    sub = lax.axis_index("sub")
    me = lax.axis_index("blk") * n_sub + sub
    after, before = lax.rem(me + 1, count), lax.rem(me + count - 1, count)
    places = [(at // n_sub, at % n_sub) for at in (after, before)]
    up, down = 0, 1
    spot = lax.rem(sub, RING)

    barrier = pltpu.get_barrier_semaphore()

    @pl.when(spot != RING - 1)
    def _():
        pl.semaphore_signal(barrier, inc=1, device_id=places[up], device_id_type=MESH)

    @pl.when(spot < 2)
    def _():
        pl.semaphore_signal(barrier, inc=1, device_id=places[down], device_id_type=MESH)

    loads = [pltpu.make_async_copy(whole, raw.at[a], load_sem.at[a]) for a, whole in enumerate((img, txt))]
    for load in loads:
        load.start()

    def send(side, k):
        return pltpu.make_async_remote_copy(
            src_ref=(img, txt)[k // steps].at[pl.ds((k % steps) * ROWS, ROWS)],
            dst_ref=arrived.at[side, k],
            send_sem=send_sem.at[side, k],
            recv_sem=recv_sem.at[side, k],
            device_id=places[side],
            device_id_type=MESH,
        )

    def start_sends(side):
        for k in range(2 * steps):
            send(side, k).start()

    @pl.when(spot == RING - 1)
    def _():
        pl.semaphore_wait(barrier, 2)
        pl.semaphore_signal(ready_sem.at[down], inc=1, device_id=places[up], device_id_type=MESH)
        pl.semaphore_signal(ready_sem.at[up], inc=1, device_id=places[down], device_id_type=MESH)
        start_sends(up)
        start_sends(down)

    @pl.when(spot != RING - 1)
    def _():
        pl.semaphore_wait(barrier, 1)

        @pl.when(spot == 0)
        def _():
            start_sends(up)

        @pl.when(spot != 0)
        def _():
            @pl.when(spot > 1)
            def _():
                pl.semaphore_signal(ready_sem.at[up], inc=1, device_id=places[down], device_id_type=MESH)

            start_sends(down)
            pl.semaphore_wait(ready_sem.at[up], 1)
            start_sends(up)

    with jax.named_scope("own_units"):
        for a in range(2):
            loads[a].wait()

            @pl.loop(0, rows // PART)
            def _(m):
                block = pl.ds(pl.multiple_of(m * PART, PART), PART)
                values, recip = unit_rows(raw[a, block])
                low[a, block] = values.astype(jnp.bfloat16)
                recips[a, block] = recip
    scale, bias = scale_ref[0], bias_ref[0]
    scalars[0] = jnp.full(scalars.shape[1:], scale, jnp.float32)
    scalars[1] = jnp.full(scalars.shape[1:], bias, jnp.float32)
    total[...] = jnp.zeros_like(total)

    def add_rows(a, some):
        for m in range(0, rows, BLOCK):
            block = pl.ds(m, BLOCK)
            total[a, block] += weighted(pair_weights(low[a, block], some, scale, bias), some)

    with jax.named_scope("own_pairs"):
        @pl.loop(0, rows // BLOCK)
        def _(j):
            first = pl.multiple_of(j * BLOCK, BLOCK)
            for a in range(2):
                some = low[1 - a, pl.ds(first, BLOCK)]
                for m in range(0, rows, BLOCK):
                    block = pl.ds(m, BLOCK)
                    weights = pair_weights(low[a, block], some, scale, bias)
                    at = lax.broadcasted_iota(jnp.int32, weights.shape, 0) + m
                    to = lax.broadcasted_iota(jnp.int32, weights.shape, 1) + first
                    total[a, block] += weighted(weights - jnp.where(at == to, 1.0, 0.0), some)

    @pl.when(spot == 0)
    def _():
        pl.semaphore_wait(ready_sem.at[down], 1)
        start_sends(down)

    last = 2 * steps - 1

    @pl.loop(0, last + 1)
    def _(k):
        a = 1 - k // steps
        with jax.named_scope("wait"):
            for side in range(2):
                pltpu.make_async_copy(arrived.at[side, k], arrived.at[side, k], recv_sem.at[side, k]).wait()
        with jax.named_scope("step"):
            for side in range(2):
                unit[pl.ds(side * ROWS, ROWS)] = unit_rows(arrived[side, k])[0].astype(jnp.bfloat16)

            @pl.when(k < last)
            def _():
                add_rows(a, unit[...])

            @pl.when(k == steps - 1)
            def _():
                @pl.loop(0, rows // PART)
                def _(m):
                    block = pl.ds(pl.multiple_of(m * PART, PART), PART)
                    total[1, block] = back_norm(raw[1, block], recips[1, block], scale * total[1, block])

    with jax.named_scope("wait_sends"):
        for k in range(2 * steps):
            for side in range(2):
                send(side, k).wait_send()


def complete(total, raw, low, recips, unit, scalars, g_img, g_txt, result, out_sem):
    rows = result.shape[0]
    whole = pltpu.make_async_copy(total.at[1], g_txt, out_sem.at[rows // PART])
    whole.start()
    scale, bias = scalars[0, 0:1, 0:1], scalars[1, 0:1, 0:1]
    some = unit[...]
    outs = []
    for m in range(rows // PART):
        block = pl.ds(m * PART, PART)
        grad = total[0, block] + weighted(pair_weights(low[0, block], some, scale, bias), some)
        result[block] = back_norm(raw[0, block], recips[0, block], scale * grad)
        outs.append(pltpu.make_async_copy(result.at[block], g_img.at[block], out_sem.at[m]))
        outs[-1].start()
    for out in outs:
        out.wait()
    whole.wait()


def solution(mesh):
    n_blk, n_sub = mesh.shape["blk"], mesh.shape["sub"]

    def step(images, texts, logit_scale, logit_bias):
        rows, width = images.shape
        steps = rows // ROWS
        vmem = pl.BlockSpec(memory_space=pltpu.VMEM)
        hbm = pl.BlockSpec(memory_space=pltpu.HBM)
        args = [logit_scale, logit_bias] + [pltpu.with_memory_space_constraint(x, pltpu.HBM) for x in (images, texts)]
        smem = pl.BlockSpec(memory_space=pltpu.SMEM)
        held = pl.pallas_call(
            functools.partial(exchange, n_blk, n_sub),
            out_shape=[
                jax.ShapeDtypeStruct((2, rows, width), jnp.float32),
                jax.ShapeDtypeStruct((2, rows, width), jnp.bfloat16),
                jax.ShapeDtypeStruct((2, rows, width), jnp.bfloat16),
                jax.ShapeDtypeStruct((2, rows, 1), jnp.float32),
                jax.ShapeDtypeStruct((2 * ROWS, width), jnp.bfloat16),
                jax.ShapeDtypeStruct((2, 8, 128), jnp.float32),
            ],
            in_specs=[smem] * 2 + [hbm] * 2,
            out_specs=[vmem] * 6,
            scratch_shapes=[
                pltpu.VMEM((2, 2 * steps, ROWS, width), jnp.bfloat16),
                pltpu.SemaphoreType.DMA((2,)),
                pltpu.SemaphoreType.DMA((2, 2 * steps)),
                pltpu.SemaphoreType.DMA((2, 2 * steps)),
                pltpu.SemaphoreType.REGULAR((2,)),
            ],
            compiler_params=pltpu.CompilerParams(
                collective_id=0, has_side_effects=True, vmem_limit_bytes=24 << 20
            ),
        )(*args)
        return pl.pallas_call(
            complete,
            out_shape=[jax.ShapeDtypeStruct((rows, width), jnp.float32)] * 2,
            in_specs=[vmem] * 6,
            out_specs=[hbm] * 2,
            scratch_shapes=[
                pltpu.VMEM((rows, width), jnp.float32),
                pltpu.SemaphoreType.DMA((rows // PART + 1,)),
            ],
            compiler_params=pltpu.CompilerParams(vmem_limit_bytes=24 << 20),
        )(*held)

    rows_spec = P(("blk", "sub"), None)
    return jax.shard_map(
        step, mesh=mesh, in_specs=(rows_spec, rows_spec, P(), P()), out_specs=(rows_spec, rows_spec), check_vma=False
    )
```

```python
import functools

import jax
import jax.numpy as jnp
from jax import lax
from jax.experimental import pallas as pl
from jax.experimental.pallas import tpu as pltpu
from jax.sharding import PartitionSpec as P

MESH = pl.DeviceIdType.MESH
RING = 8
ROWS = 128
SMALL = 64
RELAYED = (2, 4)
BLOCK = 256
PART = 128


def unit_rows(raw):
    values = raw.astype(jnp.float32)
    recip = lax.rsqrt(jnp.sum(values * values, axis=-1, keepdims=True) + 1e-06)
    return values * recip, recip


def pair_weights(own, some, scale, bias):
    dots = lax.dot_general(own, some, (((1,), (1,)), ((), ())), preferred_element_type=jnp.float32)
    return jax.nn.sigmoid(scale * dots + bias)


def weighted(weights, some):
    return jnp.dot(weights.astype(jnp.bfloat16), some, preferred_element_type=jnp.float32)


def back_norm(raw, recip, grad):
    unit = raw.astype(jnp.float32) * recip
    return (grad - unit * jnp.sum(unit * grad, axis=-1, keepdims=True)) * recip


def exchange(n_blk, n_sub, scale_ref, bias_ref, img, txt, total, raw, low, recips, final, scalars,
             arrived, unit, passing, load_sem, send_sem, recv_sem, ready_sem, relay_sem):
    count = n_blk * n_sub
    rows = img.shape[0]
    steps = rows // ROWS
    blk, sub = lax.axis_index("blk"), lax.axis_index("sub")
    me = blk * n_sub + sub
    after, before = lax.rem(me + 1, count), lax.rem(me + count - 1, count)
    places = [(at // n_sub, at % n_sub) for at in (after, before)]
    up, down = 0, 1
    spot = lax.rem(sub, RING)
    core, part = lax.rem(blk, 2), lax.rem(blk // 2, 3)
    first = sub == 0
    early = first & ((core == 1) | (part == 0))
    yields = [first & (core == 1) & (part == 2), first & (core == 0) & (part != 0)]
    sender = (core == 1) & (part == 2) & (sub == n_sub - 1) & (blk != n_blk - 1)
    relays = [
        (core == 1) & (part == 0) & (sub == RING) & (blk != 1),
        (core == 1) & (part == 2) & (sub == 2 * RING) & (blk != n_blk - 1),
    ]
    taker = first & (core == 0) & (part == 0) & (blk != 0)
    relay = relays[0] | relays[1]
    sender_place = (jnp.where(relays[0], blk - 2, blk), n_sub - 1)
    relay_places = [(blk + 2, RING), (blk, 2 * RING)]
    taker_place = (jnp.where(relays[0], blk - 1, blk + 1), 0)
    taken_places = [(blk + 1, RING), (blk - 1, 2 * RING)]
    pieces = [(k * ROWS, ROWS) for k in range(2 * steps - 1)]
    pieces += [(2 * rows - 2 * SMALL, SMALL), (2 * rows - SMALL, SMALL)]

    barrier = pltpu.get_barrier_semaphore()

    @pl.when(spot != RING - 1)
    def _():
        pl.semaphore_signal(barrier, inc=1, device_id=places[up], device_id_type=MESH)

    @pl.when(spot < 2)
    def _():
        pl.semaphore_signal(barrier, inc=1, device_id=places[down], device_id_type=MESH)

    @pl.when(relay)
    def _():
        pl.semaphore_signal(barrier, inc=1, device_id=sender_place, device_id_type=MESH)

    @pl.when(taker)
    def _():
        for place in taken_places:
            pl.semaphore_signal(barrier, inc=1, device_id=place, device_id_type=MESH)

    loads = [pltpu.make_async_copy(whole, raw.at[a], load_sem.at[a]) for a, whole in enumerate((img, txt))]
    for load in loads:
        load.start()

    def send(side, k, dst, recv, place):
        at, size = pieces[k]
        pltpu.make_async_remote_copy(
            src_ref=(img, txt)[at // rows].at[pl.ds(at % rows, size)],
            dst_ref=dst,
            send_sem=send_sem.at[side],
            recv_sem=recv,
            device_id=place,
            device_id_type=MESH,
        ).start()

    def start_sends(side, skipped=(), begin=0, end=len(pieces)):
        for k, piece in list(enumerate(pieces))[begin:end]:
            if k not in skipped:
                send(side, k, arrived.at[side, pl.ds(*piece)], recv_sem.at[side, k], places[side])

    def onward(k):
        return pltpu.make_async_remote_copy(
            src_ref=passing,
            dst_ref=arrived.at[up, pl.ds(*pieces[k])],
            send_sem=relay_sem.at[1],
            recv_sem=recv_sem.at[up, k],
            device_id=taker_place,
            device_id_type=MESH,
        )

    def answered_sends(end=len(pieces)):
        pl.semaphore_wait(ready_sem.at[down], 1)
        start_sends(down, end=end)

    @pl.when(spot == RING - 1)
    def _():
        pl.semaphore_wait(barrier, jnp.where(sender, 2 + len(RELAYED), 2))
        pl.semaphore_signal(ready_sem.at[down], inc=1, device_id=places[up], device_id_type=MESH)
        pl.semaphore_signal(ready_sem.at[up], inc=1, device_id=places[down], device_id_type=MESH)

        @pl.when(sender)
        def _():
            send(up, RELAYED[0], passing, relay_sem.at[0], relay_places[0])
            start_sends(up, RELAYED, 0, 1)
            send(up, RELAYED[1], passing, relay_sem.at[0], relay_places[1])
            start_sends(up, RELAYED, 1)

        @pl.when(jnp.logical_not(sender))
        def _():
            start_sends(up)

        start_sends(down)

    @pl.when(spot != RING - 1)
    def _():
        pl.semaphore_wait(barrier, jnp.where(relay, 2, 1))

        @pl.when(spot == 0)
        def _():
            start_sends(up)

        @pl.when(spot != 0)
        def _():
            @pl.when(spot > 1)
            def _():
                pl.semaphore_signal(ready_sem.at[up], inc=1, device_id=places[down], device_id_type=MESH)

            start_sends(down)
            pl.semaphore_wait(ready_sem.at[up], 1)
            start_sends(up)

    with jax.named_scope("own_units"):
        for a in range(2):
            loads[a].wait()

            @pl.loop(0, rows // PART)
            def _(m):
                block = pl.ds(pl.multiple_of(m * PART, PART), PART)
                values, recip = unit_rows(raw[a, block])
                low[a, block] = values.astype(jnp.bfloat16)
                recips[a, block] = recip
    pl.when((spot == 0) & jnp.logical_not(early | relays[0] | yields[1]))(answered_sends)
    pl.when(relays[0])(lambda: answered_sends(5))
    pl.when(yields[1])(lambda: answered_sends(4))
    scale, bias = scale_ref[0], bias_ref[0]
    scalars[0] = jnp.full(scalars.shape[1:], scale, jnp.float32)
    scalars[1] = jnp.full(scalars.shape[1:], bias, jnp.float32)
    total[...] = jnp.zeros_like(total)

    def add_rows(a, some):
        blocks = [pl.ds(m, BLOCK) for m in range(0, rows, BLOCK)]
        weights = [pair_weights(low[a, block], some, scale, bias).astype(jnp.bfloat16) for block in blocks]
        for block, part in zip(blocks, weights):
            total[a, block] += weighted(part, some)

    with jax.named_scope("own_pairs"):
        @pl.loop(0, rows // BLOCK)
        def _(j):
            begin = pl.multiple_of(j * BLOCK, BLOCK)
            for a in range(2):
                some = low[1 - a, pl.ds(begin, BLOCK)]
                for m in range(0, rows, BLOCK):
                    block = pl.ds(m, BLOCK)
                    weights = pair_weights(low[a, block], some, scale, bias)
                    at = lax.broadcasted_iota(jnp.int32, weights.shape, 0) + m
                    to = lax.broadcasted_iota(jnp.int32, weights.shape, 1) + begin
                    total[a, block] += weighted(weights - jnp.where(at == to, 1.0, 0.0), some)

    pl.when(early & jnp.logical_not(yields[0]))(answered_sends)
    pl.when(yields[0])(lambda: answered_sends(3))

    def receive(k, at, size, into):
        for side in range(2):
            there = arrived.at[side, pl.ds(at, size)]
            with jax.named_scope("wait"):
                pltpu.make_async_copy(there, there, recv_sem.at[side, k]).wait()
            into[pl.ds(side * size, size)] = unit_rows(there[...])[0].astype(jnp.bfloat16)

    @pl.loop(0, 2 * steps - 1)
    def _(k):
        receive(k, pl.multiple_of(k * ROWS, ROWS), ROWS, unit)
        with jax.named_scope("step"):
            add_rows(1 - k // steps, unit[...])

        pl.when(yields[0] & (k == 3))(lambda: start_sends(down, begin=3))
        pl.when(yields[1] & (k == 3))(lambda: start_sends(down, begin=4))

        def pass_on(m):
            pltpu.make_async_copy(passing, passing, relay_sem.at[0]).wait()
            onward(RELAYED[m]).start()

        @pl.when(relays[0] & (k == 3))
        def _():
            pass_on(0)
            start_sends(down, begin=5)

        pl.when(relays[1] & (k == 1))(lambda: pass_on(1))

        @pl.when(k == steps - 1)
        def _():
            @pl.loop(0, rows // PART)
            def _(m):
                block = pl.ds(pl.multiple_of(m * PART, PART), PART)
                total[1, block] = back_norm(raw[1, block], recips[1, block], scale * total[1, block])


    k = 2 * steps - 1
    receive(k, *pieces[k], unit)
    with jax.named_scope("small"):
        add_rows(0, unit[: 2 * SMALL])
    receive(k + 1, *pieces[k + 1], final)
    with jax.named_scope("wait_sends"):
        for side in range(2):
            pltpu.make_async_copy(arrived.at[side], arrived.at[side], send_sem.at[side]).wait()
    pl.when(relay)(onward(RELAYED[0]).wait_send)


def complete(total, raw, low, recips, final, scalars, g_img, g_txt, result, out_sem):
    rows = result.shape[0]
    whole = pltpu.make_async_copy(total.at[1], g_txt, out_sem.at[rows // PART])
    whole.start()
    scale, bias = scalars[0, 0:1, 0:1], scalars[1, 0:1, 0:1]
    some = final[...]
    outs = [whole]
    for at in range(0, rows, BLOCK):
        weights = pair_weights(low[0, pl.ds(at, BLOCK)], some, scale, bias)
        for m in range(at // PART, (at + BLOCK) // PART):
            block = pl.ds(m * PART, PART)
            grad = total[0, block] + weighted(weights[m * PART - at : (m + 1) * PART - at], some)
            result[block] = back_norm(raw[0, block], recips[0, block], scale * grad)
            outs.append(pltpu.make_async_copy(result.at[block], g_img.at[block], out_sem.at[m]))
            outs[-1].start()
    for out in outs:
        out.wait()


def solution(mesh):
    n_blk, n_sub = mesh.shape["blk"], mesh.shape["sub"]

    def step(images, texts, logit_scale, logit_bias):
        rows, width = images.shape
        steps = rows // ROWS
        vmem = pl.BlockSpec(memory_space=pltpu.VMEM)
        hbm = pl.BlockSpec(memory_space=pltpu.HBM)
        args = [logit_scale, logit_bias] + [pltpu.with_memory_space_constraint(x, pltpu.HBM) for x in (images, texts)]
        smem = pl.BlockSpec(memory_space=pltpu.SMEM)
        held = pl.pallas_call(
            functools.partial(exchange, n_blk, n_sub),
            out_shape=[
                jax.ShapeDtypeStruct((2, rows, width), jnp.float32),
                jax.ShapeDtypeStruct((2, rows, width), jnp.bfloat16),
                jax.ShapeDtypeStruct((2, rows, width), jnp.bfloat16),
                jax.ShapeDtypeStruct((2, rows, 1), jnp.float32),
                jax.ShapeDtypeStruct((2 * SMALL, width), jnp.bfloat16),
                jax.ShapeDtypeStruct((2, 8, 128), jnp.float32),
            ],
            in_specs=[smem] * 2 + [hbm] * 2,
            out_specs=[vmem] * 6,
            scratch_shapes=[
                pltpu.VMEM((2, 2 * rows, width), jnp.bfloat16),
                pltpu.VMEM((2 * ROWS, width), jnp.bfloat16),
                pltpu.VMEM((ROWS, width), jnp.bfloat16),
                pltpu.SemaphoreType.DMA((2,)),
                pltpu.SemaphoreType.DMA((2,)),
                pltpu.SemaphoreType.DMA((2, 2 * steps + 1)),
                pltpu.SemaphoreType.REGULAR((2,)),
                pltpu.SemaphoreType.DMA((2,)),
            ],
            compiler_params=pltpu.CompilerParams(
                collective_id=0, has_side_effects=True, vmem_limit_bytes=24 << 20
            ),
        )(*args)
        return pl.pallas_call(
            complete,
            out_shape=[jax.ShapeDtypeStruct((rows, width), jnp.float32)] * 2,
            in_specs=[vmem] * 6,
            out_specs=[hbm] * 2,
            scratch_shapes=[
                pltpu.VMEM((rows, width), jnp.float32),
                pltpu.SemaphoreType.DMA((rows // PART + 1,)),
            ],
            compiler_params=pltpu.CompilerParams(vmem_limit_bytes=24 << 20),
        )(*held)

    rows_spec = P(("blk", "sub"), None)
    return jax.shard_map(
        step, mesh=mesh, in_specs=(rows_spec, rows_spec, P(), P()), out_specs=(rows_spec, rows_spec), check_vma=False
    )
```

```python
import functools

import jax
import jax.numpy as jnp
from jax import lax
from jax.experimental import pallas as pl
from jax.experimental.pallas import tpu as pltpu
from jax.sharding import PartitionSpec as P

MESH = pl.DeviceIdType.MESH
RING = 8
ROWS = 128
SMALL = 64
RELAYED = (2, 4)
BLOCK = 256
PART = 128


def unit_rows(raw):
    values = raw.astype(jnp.float32)
    recip = lax.rsqrt(jnp.sum(values * values, axis=-1, keepdims=True) + 1e-06)
    return values * recip, recip


def pair_weights(own, some, scale, bias):
    dots = lax.dot_general(own, some, (((1,), (1,)), ((), ())), preferred_element_type=jnp.float32)
    return jax.nn.sigmoid(scale * dots + bias)


def weighted(weights, some):
    return jnp.dot(weights.astype(jnp.bfloat16), some, preferred_element_type=jnp.float32)


def back_norm(raw, recip, grad):
    unit = raw.astype(jnp.float32) * recip
    return (grad - unit * jnp.sum(unit * grad, axis=-1, keepdims=True)) * recip


def exchange(n_blk, n_sub, scale_ref, bias_ref, img, txt, total, raw, low, recips, final, scalars,
             arrived, unit, passing, load_sem, send_sem, recv_sem, ready_sem, relay_sem):
    rows = img.shape[0]
    steps = rows // ROWS
    blk, sub = lax.axis_index("blk"), lax.axis_index("sub")
    first, ended = sub == 0, sub == n_sub - 1
    next_blk, last_blk = jnp.where(blk == n_blk - 1, 0, blk + 1), jnp.where(blk == 0, n_blk - 1, blk - 1)
    places = [
        (jnp.where(ended, next_blk, blk), jnp.where(ended, 0, sub + 1)),
        (jnp.where(first, last_blk, blk), jnp.where(first, n_sub - 1, sub - 1)),
    ]
    up, down = 0, 1
    spot = lax.rem(sub, RING)
    pair, core = blk // 2, blk % 2
    part = pair - (pair * 11 // 32) * 3
    early = first & ((core == 1) | (part == 0))
    yields = [first & (core == 1) & (part == 2), first & (core == 0) & (part != 0)]
    near = ended & (core == 1) & (part != 2)
    sender = ended & (core == 1) & (part == 2) & (blk != n_blk - 1)
    relays = [
        (core == 1) & (part == 0) & (sub == RING) & (blk != 1),
        (core == 1) & (part == 2) & (sub == 2 * RING) & (blk != n_blk - 1),
    ]
    taker = first & (core == 0) & (part == 0) & (blk != 0)
    relay = relays[0] | relays[1]
    sender_place = (jnp.where(relays[0], blk - 2, blk), n_sub - 1)
    relay_places = [(blk + 2, RING), (blk, 2 * RING)]
    taker_place = (jnp.where(relays[0], blk - 1, blk + 1), 0)
    taken_places = [(blk + 1, RING), (blk - 1, 2 * RING)]
    pieces = [(k * ROWS, ROWS) for k in range(2 * steps - 1)]
    pieces += [(2 * rows - 2 * SMALL, SMALL), (2 * rows - SMALL, SMALL)]

    barrier = pltpu.get_barrier_semaphore()

    @pl.when((spot != RING - 1) | near)
    def _():
        pl.semaphore_signal(barrier, inc=1, device_id=places[up], device_id_type=MESH)

    @pl.when(spot < 2)
    def _():
        pl.semaphore_signal(barrier, inc=1, device_id=places[down], device_id_type=MESH)

    @pl.when(relay)
    def _():
        pl.semaphore_signal(barrier, inc=1, device_id=sender_place, device_id_type=MESH)

    @pl.when(taker)
    def _():
        for place in taken_places:
            pl.semaphore_signal(barrier, inc=1, device_id=place, device_id_type=MESH)

    loads = [pltpu.make_async_copy(whole, raw.at[a], load_sem.at[a]) for a, whole in enumerate((img, txt))]
    def send(side, k, dst, recv, place):
        at, size = pieces[k]
        pltpu.make_async_remote_copy(
            src_ref=(img, txt)[at // rows].at[pl.ds(at % rows, size)],
            dst_ref=dst,
            send_sem=send_sem.at[side],
            recv_sem=recv,
            device_id=place,
            device_id_type=MESH,
        ).start()

    def start_sends(side, skipped=(), begin=0, end=len(pieces)):
        for k, piece in list(enumerate(pieces))[begin:end]:
            if k not in skipped:
                send(side, k, arrived.at[side, pl.ds(*piece)], recv_sem.at[side, k], places[side])

    def onward(k):
        return pltpu.make_async_remote_copy(
            src_ref=passing,
            dst_ref=arrived.at[up, pl.ds(*pieces[k])],
            send_sem=relay_sem.at[1],
            recv_sem=recv_sem.at[up, k],
            device_id=taker_place,
            device_id_type=MESH,
        )

    def answered_sends(end=len(pieces)):
        pl.semaphore_wait(ready_sem.at[down], 1)
        start_sends(down, end=end)

    @pl.when(spot == RING - 1)
    def _():
        pl.semaphore_wait(barrier, jnp.where(sender, 2 + len(RELAYED), 2))

        @pl.when(jnp.logical_not(near))
        def _():
            pl.semaphore_signal(ready_sem.at[down], inc=1, device_id=places[up], device_id_type=MESH)

        pl.semaphore_signal(ready_sem.at[up], inc=1, device_id=places[down], device_id_type=MESH)

        @pl.when(sender)
        def _():
            send(up, RELAYED[0], passing, relay_sem.at[0], relay_places[0])
            start_sends(up, RELAYED, 0, 1)
            send(up, RELAYED[1], passing, relay_sem.at[0], relay_places[1])
            start_sends(up, RELAYED, 1)

        @pl.when(jnp.logical_not(sender))
        def _():
            start_sends(up)

        start_sends(down)

    @pl.when(spot != RING - 1)
    def _():
        pl.semaphore_wait(barrier, jnp.where(relay | yields[1], 2, 1))

        @pl.when(spot == 0)
        def _():
            start_sends(up)
            pl.when(yields[1])(lambda: start_sends(down, end=4))

        @pl.when(spot != 0)
        def _():
            @pl.when(spot > 1)
            def _():
                pl.semaphore_signal(ready_sem.at[up], inc=1, device_id=places[down], device_id_type=MESH)

            start_sends(down)
            pl.semaphore_wait(ready_sem.at[up], 1)
            start_sends(up)

    for load in loads:
        load.start()

    with jax.named_scope("own_units"):
        for a in range(2):
            loads[a].wait()

            @pl.loop(0, rows // PART)
            def _(m):
                block = pl.ds(pl.multiple_of(m * PART, PART), PART)
                values, recip = unit_rows(raw[a, block])
                low[a, block] = values.astype(jnp.bfloat16)
                recips[a, block] = recip
    pl.when((spot == 0) & jnp.logical_not(early | relays[0] | yields[1]))(answered_sends)
    pl.when(relays[0])(lambda: answered_sends(5))
    scale, bias = scale_ref[0], bias_ref[0]
    scalars[0] = jnp.full(scalars.shape[1:], scale, jnp.float32)
    scalars[1] = jnp.full(scalars.shape[1:], bias, jnp.float32)
    total[...] = jnp.zeros_like(total)

    def add_rows(a, some):
        blocks = [pl.ds(m, BLOCK) for m in range(0, rows, BLOCK)]
        weights = [pair_weights(low[a, block], some, scale, bias).astype(jnp.bfloat16) for block in blocks]
        for block, part in zip(blocks, weights):
            total[a, block] += weighted(part, some)

    with jax.named_scope("own_pairs"):
        @pl.loop(0, rows // BLOCK)
        def _(j):
            begin = pl.multiple_of(j * BLOCK, BLOCK)
            for a in range(2):
                some = low[1 - a, pl.ds(begin, BLOCK)]
                for m in range(0, rows, BLOCK):
                    block = pl.ds(m, BLOCK)
                    weights = pair_weights(low[a, block], some, scale, bias)
                    at = lax.broadcasted_iota(jnp.int32, weights.shape, 0) + m
                    to = lax.broadcasted_iota(jnp.int32, weights.shape, 1) + begin
                    total[a, block] += weighted(weights - jnp.where(at == to, 1.0, 0.0), some)

    pl.when(early & jnp.logical_not(yields[0]))(answered_sends)
    pl.when(yields[0])(lambda: answered_sends(3))

    def receive(k, at, size, into):
        for side in range(2):
            there = arrived.at[side, pl.ds(at, size)]
            with jax.named_scope("wait"):
                pltpu.make_async_copy(there, there, recv_sem.at[side, k]).wait()
            into[pl.ds(side * size, size)] = unit_rows(there[...])[0].astype(jnp.bfloat16)

    def pass_on(m):
        pltpu.make_async_copy(passing, passing, relay_sem.at[0]).wait()
        onward(RELAYED[m]).start()

    @pl.loop(0, 2 * steps - 1)
    def _(k):
        receive(k, pl.multiple_of(k * ROWS, ROWS), ROWS, unit)
        pl.when(yields[0] & (k == 3))(lambda: start_sends(down, begin=3))
        pl.when(yields[1] & (k == 3))(lambda: start_sends(down, begin=4))

        @pl.when(relays[0] & (k == 3))
        def _():
            pass_on(0)
            start_sends(down, begin=5)

        pl.when(relays[1] & (k == 1))(lambda: pass_on(1))

        with jax.named_scope("step"):
            add_rows(1 - k // steps, unit[...])

        @pl.when(k == steps - 1)
        def _():
            @pl.loop(0, rows // PART)
            def _(m):
                block = pl.ds(pl.multiple_of(m * PART, PART), PART)
                total[1, block] = back_norm(raw[1, block], recips[1, block], scale * total[1, block])


    k = 2 * steps - 1
    receive(k, *pieces[k], unit)
    with jax.named_scope("small"):
        add_rows(0, unit[: 2 * SMALL])
    receive(k + 1, *pieces[k + 1], final)
    with jax.named_scope("wait_sends"):
        for side in range(2):
            pltpu.make_async_copy(arrived.at[side], arrived.at[side], send_sem.at[side]).wait()
    pl.when(relay)(onward(RELAYED[0]).wait_send)


def complete(total, raw, low, recips, final, scalars, g_img, g_txt, result, out_sem):
    rows = result.shape[0]
    whole = pltpu.make_async_copy(total.at[1], g_txt, out_sem.at[rows // PART])
    whole.start()
    scale, bias = scalars[0, 0:1, 0:1], scalars[1, 0:1, 0:1]
    some = final[...]
    outs = [whole]
    for at in range(0, rows, BLOCK):
        weights = pair_weights(low[0, pl.ds(at, BLOCK)], some, scale, bias)
        for m in range(at // PART, (at + BLOCK) // PART):
            block = pl.ds(m * PART, PART)
            grad = total[0, block] + weighted(weights[m * PART - at : (m + 1) * PART - at], some)
            result[block] = back_norm(raw[0, block], recips[0, block], scale * grad)
            outs.append(pltpu.make_async_copy(result.at[block], g_img.at[block], out_sem.at[m]))
            outs[-1].start()
    for out in outs:
        out.wait()


def solution(mesh):
    n_blk, n_sub = mesh.shape["blk"], mesh.shape["sub"]

    def step(images, texts, logit_scale, logit_bias):
        rows, width = images.shape
        steps = rows // ROWS
        vmem = pl.BlockSpec(memory_space=pltpu.VMEM)
        hbm = pl.BlockSpec(memory_space=pltpu.HBM)
        args = [logit_scale, logit_bias] + [pltpu.with_memory_space_constraint(x, pltpu.HBM) for x in (images, texts)]
        smem = pl.BlockSpec(memory_space=pltpu.SMEM)
        held = pl.pallas_call(
            functools.partial(exchange, n_blk, n_sub),
            out_shape=[
                jax.ShapeDtypeStruct((2, rows, width), jnp.float32),
                jax.ShapeDtypeStruct((2, rows, width), jnp.bfloat16),
                jax.ShapeDtypeStruct((2, rows, width), jnp.bfloat16),
                jax.ShapeDtypeStruct((2, rows, 1), jnp.float32),
                jax.ShapeDtypeStruct((2 * SMALL, width), jnp.bfloat16),
                jax.ShapeDtypeStruct((2, 8, 128), jnp.float32),
            ],
            in_specs=[smem] * 2 + [hbm] * 2,
            out_specs=[vmem] * 6,
            scratch_shapes=[
                pltpu.VMEM((2, 2 * rows, width), jnp.bfloat16),
                pltpu.VMEM((2 * ROWS, width), jnp.bfloat16),
                pltpu.VMEM((ROWS, width), jnp.bfloat16),
                pltpu.SemaphoreType.DMA((2,)),
                pltpu.SemaphoreType.DMA((2,)),
                pltpu.SemaphoreType.DMA((2, 2 * steps + 1)),
                pltpu.SemaphoreType.REGULAR((2,)),
                pltpu.SemaphoreType.DMA((2,)),
            ],
            compiler_params=pltpu.CompilerParams(
                collective_id=0, has_side_effects=True, vmem_limit_bytes=24 << 20
            ),
        )(*args)
        return pl.pallas_call(
            complete,
            out_shape=[jax.ShapeDtypeStruct((rows, width), jnp.float32)] * 2,
            in_specs=[vmem] * 6,
            out_specs=[hbm] * 2,
            scratch_shapes=[
                pltpu.VMEM((rows, width), jnp.float32),
                pltpu.SemaphoreType.DMA((rows // PART + 1,)),
            ],
            compiler_params=pltpu.CompilerParams(vmem_limit_bytes=24 << 20),
        )(*held)

    rows_spec = P(("blk", "sub"), None)
    return jax.shard_map(
        step, mesh=mesh, in_specs=(rows_spec, rows_spec, P(), P()), out_specs=(rows_spec, rows_spec), check_vma=False
    )
```

```python
import functools

import jax
import jax.numpy as jnp
from jax import lax
from jax.experimental import pallas as pl
from jax.experimental.pallas import tpu as pltpu
from jax.sharding import PartitionSpec as P

MESH = pl.DeviceIdType.MESH
RING = 8
ROWS = 128
SMALL = 64
RELAYED = (2, 4)
BLOCK = 256
PART = 128


def unit_rows(raw):
    values = raw.astype(jnp.float32)
    recip = lax.rsqrt(jnp.sum(values * values, axis=-1, keepdims=True) + 1e-06)
    return values * recip, recip


def pair_weights(own, some, scale, bias):
    dots = lax.dot_general(own, some, (((1,), (1,)), ((), ())), preferred_element_type=jnp.float32)
    return jax.nn.sigmoid(scale * dots + bias)


def weighted(weights, some):
    return jnp.dot(weights.astype(jnp.bfloat16), some, preferred_element_type=jnp.float32)


def back_norm(raw, recip, grad):
    unit = raw.astype(jnp.float32) * recip
    return (grad - unit * jnp.sum(unit * grad, axis=-1, keepdims=True)) * recip


def exchange(n_blk, n_sub, scale_ref, bias_ref, img, txt, total, raw, low, recips, final, scalars,
             arrived, unit, passing, load_sem, send_sem, recv_sem, ready_sem, relay_sem):
    rows = img.shape[0]
    steps = rows // ROWS
    blk, sub = lax.axis_index("blk"), lax.axis_index("sub")
    first, ended = sub == 0, sub == n_sub - 1
    next_blk, last_blk = jnp.where(blk == n_blk - 1, 0, blk + 1), jnp.where(blk == 0, n_blk - 1, blk - 1)
    places = [
        (jnp.where(ended, next_blk, blk), jnp.where(ended, 0, sub + 1)),
        (jnp.where(first, last_blk, blk), jnp.where(first, n_sub - 1, sub - 1)),
    ]
    up, down = 0, 1
    spot = lax.rem(sub, RING)
    pair, core = blk // 2, blk % 2
    part = pair - (pair * 11 // 32) * 3
    early = first & ((core == 1) | (part == 0))
    yields = [first & (core == 1) & (part == 2), first & (core == 0) & (part != 0)]
    near = ended & (core == 1) & (part != 2)
    sender = ended & (core == 1) & (part == 2) & (blk != n_blk - 1)
    relays = [
        (core == 1) & (part == 0) & (sub == RING) & (blk != 1),
        (core == 1) & (part == 2) & (sub == 2 * RING) & (blk != n_blk - 1),
    ]
    taker = first & (core == 0) & (part == 0) & (blk != 0)
    relay = relays[0] | relays[1]
    sender_place = (jnp.where(relays[0], blk - 2, blk), n_sub - 1)
    relay_places = [(blk + 2, RING), (blk, 2 * RING)]
    taker_place = (jnp.where(relays[0], blk - 1, blk + 1), 0)
    taken_places = [(blk + 1, RING), (blk - 1, 2 * RING)]
    pieces = [(k * ROWS, ROWS) for k in range(2 * steps - 1)]
    pieces += [(2 * rows - 2 * SMALL, SMALL), (2 * rows - SMALL, SMALL)]

    barrier = pltpu.get_barrier_semaphore()

    @pl.when((spot != RING - 1) | near)
    def _():
        pl.semaphore_signal(barrier, inc=1, device_id=places[up], device_id_type=MESH)

    @pl.when(spot < 2)
    def _():
        pl.semaphore_signal(barrier, inc=1, device_id=places[down], device_id_type=MESH)

    @pl.when(relay)
    def _():
        pl.semaphore_signal(barrier, inc=1, device_id=sender_place, device_id_type=MESH)

    @pl.when(taker)
    def _():
        for place in taken_places:
            pl.semaphore_signal(barrier, inc=1, device_id=place, device_id_type=MESH)

    loads = [pltpu.make_async_copy(whole, raw.at[a], load_sem.at[a]) for a, whole in enumerate((img, txt))]
    def send(side, k, dst, recv, place):
        at, size = pieces[k]
        pltpu.make_async_remote_copy(
            src_ref=(img, txt)[at // rows].at[pl.ds(at % rows, size)],
            dst_ref=dst,
            send_sem=send_sem.at[side],
            recv_sem=recv,
            device_id=place,
            device_id_type=MESH,
        ).start()

    def start_sends(side, skipped=(), begin=0, end=len(pieces)):
        for k, piece in list(enumerate(pieces))[begin:end]:
            if k not in skipped:
                send(side, k, arrived.at[side, pl.ds(*piece)], recv_sem.at[side, k], places[side])

    def onward(k):
        return pltpu.make_async_remote_copy(
            src_ref=passing,
            dst_ref=arrived.at[up, pl.ds(*pieces[k])],
            send_sem=relay_sem.at[1],
            recv_sem=recv_sem.at[up, k],
            device_id=taker_place,
            device_id_type=MESH,
        )

    def answered_sends(end=len(pieces)):
        pl.semaphore_wait(ready_sem.at[down], 1)
        start_sends(down, end=end)

    @pl.when(spot == RING - 1)
    def _():
        pl.semaphore_wait(barrier, jnp.where(sender, 2 + len(RELAYED), 2))

        @pl.when(jnp.logical_not(near))
        def _():
            pl.semaphore_signal(ready_sem.at[down], inc=1, device_id=places[up], device_id_type=MESH)

        pl.semaphore_signal(ready_sem.at[up], inc=1, device_id=places[down], device_id_type=MESH)

        @pl.when(sender)
        def _():
            send(up, RELAYED[0], passing, relay_sem.at[0], relay_places[0])
            start_sends(up, RELAYED, 0, 1)
            send(up, RELAYED[1], passing, relay_sem.at[0], relay_places[1])
            start_sends(up, RELAYED, 1)

        @pl.when(jnp.logical_not(sender))
        def _():
            start_sends(up)

        start_sends(down)

    @pl.when(spot != RING - 1)
    def _():
        pl.semaphore_wait(barrier, jnp.where(relay | yields[1], 2, 1))

        @pl.when(spot == 0)
        def _():
            start_sends(up)
            pl.when(yields[1])(lambda: start_sends(down, end=4))

        @pl.when(spot != 0)
        def _():
            @pl.when(spot > 1)
            def _():
                pl.semaphore_signal(ready_sem.at[up], inc=1, device_id=places[down], device_id_type=MESH)

            start_sends(down)
            pl.semaphore_wait(ready_sem.at[up], 1)
            start_sends(up)

    for load in loads:
        load.start()

    with jax.named_scope("own_units"):
        for a in range(2):
            loads[a].wait()

            @pl.loop(0, rows // PART)
            def _(m):
                block = pl.ds(pl.multiple_of(m * PART, PART), PART)
                values, recip = unit_rows(raw[a, block])
                low[a, block] = values.astype(jnp.bfloat16)
                recips[a, block] = recip
    pl.when((spot == 0) & jnp.logical_not(early | relays[0] | yields[1]))(answered_sends)
    pl.when(relays[0])(lambda: answered_sends(5))
    scale, bias = scale_ref[0], bias_ref[0]
    scalars[0] = jnp.full(scalars.shape[1:], scale, jnp.float32)
    scalars[1] = jnp.full(scalars.shape[1:], bias, jnp.float32)
    total[...] = jnp.zeros_like(total)

    def add_rows(a, some):
        blocks = [pl.ds(m, BLOCK) for m in range(0, rows, BLOCK)]
        weights = [pair_weights(low[a, block], some, scale, bias).astype(jnp.bfloat16) for block in blocks]
        for block, part in zip(blocks, weights):
            total[a, block] += weighted(part, some)

    with jax.named_scope("own_pairs"):
        @pl.loop(0, rows // BLOCK)
        def _(j):
            begin = pl.multiple_of(j * BLOCK, BLOCK)
            for a in range(2):
                some = low[1 - a, pl.ds(begin, BLOCK)]
                for m in range(0, rows, BLOCK):
                    block = pl.ds(m, BLOCK)
                    weights = pair_weights(low[a, block], some, scale, bias)
                    at = lax.broadcasted_iota(jnp.int32, weights.shape, 0) + m
                    to = lax.broadcasted_iota(jnp.int32, weights.shape, 1) + begin
                    total[a, block] += weighted(weights - jnp.where(at == to, 1.0, 0.0), some)

    pl.when(early & jnp.logical_not(yields[0]))(answered_sends)
    pl.when(yields[0])(lambda: answered_sends(3))

    def receive(k, at, size, into):
        for side in range(2):
            there = arrived.at[side, pl.ds(at, size)]
            with jax.named_scope("wait"):
                pltpu.make_async_copy(there, there, recv_sem.at[side, k]).wait()
            into[pl.ds(side * size, size)] = unit_rows(there[...])[0].astype(jnp.bfloat16)

    def pass_on(m):
        pltpu.make_async_copy(passing, passing, relay_sem.at[0]).wait()
        onward(RELAYED[m]).start()

    @pl.loop(0, 2 * steps - 1)
    def _(k):
        receive(k, pl.multiple_of(k * ROWS, ROWS), ROWS, unit)
        pl.when(yields[0] & (k == 3))(lambda: start_sends(down, begin=3))
        pl.when(yields[1] & (k == 3))(lambda: start_sends(down, begin=4))

        @pl.when(relays[0] & (k == 3))
        def _():
            pass_on(0)
            start_sends(down, begin=5)

        pl.when(relays[1] & (k == 1))(lambda: pass_on(1))

        with jax.named_scope("step"):
            add_rows(1 - k // steps, unit[...])

        @pl.when(k == steps - 1)
        def _():
            @pl.loop(0, rows // PART)
            def _(m):
                block = pl.ds(pl.multiple_of(m * PART, PART), PART)
                total[1, block] = back_norm(raw[1, block], recips[1, block], scale * total[1, block])


    k = 2 * steps - 1
    receive(k, *pieces[k], unit)
    with jax.named_scope("small"):
        add_rows(0, unit[: 2 * SMALL])
    receive(k + 1, *pieces[k + 1], final)
    with jax.named_scope("wait_sends"):
        for side in range(2):
            pltpu.make_async_copy(arrived.at[side], arrived.at[side], send_sem.at[side]).wait()
    pl.when(relay)(onward(RELAYED[0]).wait_send)


def complete(total, raw, low, recips, final, scalars, g_img, g_txt, result, out_sem):
    rows = result.shape[0]
    whole = pltpu.make_async_copy(total.at[1], g_txt, out_sem.at[rows // PART])
    whole.start()
    scale, bias = scalars[0, 0:1, 0:1], scalars[1, 0:1, 0:1]
    some = final[...]
    outs = [whole]
    for m in range(rows // PART):
        block = pl.ds(m * PART, PART)
        grad = total[0, block] + weighted(pair_weights(low[0, block], some, scale, bias), some)
        result[block] = back_norm(raw[0, block], recips[0, block], scale * grad)
        outs.append(pltpu.make_async_copy(result.at[block], g_img.at[block], out_sem.at[m]))
        outs[-1].start()
    for out in outs:
        out.wait()


def solution(mesh):
    n_blk, n_sub = mesh.shape["blk"], mesh.shape["sub"]

    def step(images, texts, logit_scale, logit_bias):
        rows, width = images.shape
        steps = rows // ROWS
        vmem = pl.BlockSpec(memory_space=pltpu.VMEM)
        hbm = pl.BlockSpec(memory_space=pltpu.HBM)
        args = [logit_scale, logit_bias] + [pltpu.with_memory_space_constraint(x, pltpu.HBM) for x in (images, texts)]
        smem = pl.BlockSpec(memory_space=pltpu.SMEM)
        held = pl.pallas_call(
            functools.partial(exchange, n_blk, n_sub),
            out_shape=[
                jax.ShapeDtypeStruct((2, rows, width), jnp.float32),
                jax.ShapeDtypeStruct((2, rows, width), jnp.bfloat16),
                jax.ShapeDtypeStruct((2, rows, width), jnp.bfloat16),
                jax.ShapeDtypeStruct((2, rows, 1), jnp.float32),
                jax.ShapeDtypeStruct((2 * SMALL, width), jnp.bfloat16),
                jax.ShapeDtypeStruct((2, 8, 128), jnp.float32),
            ],
            in_specs=[smem] * 2 + [hbm] * 2,
            out_specs=[vmem] * 6,
            scratch_shapes=[
                pltpu.VMEM((2, 2 * rows, width), jnp.bfloat16),
                pltpu.VMEM((2 * ROWS, width), jnp.bfloat16),
                pltpu.VMEM((ROWS, width), jnp.bfloat16),
                pltpu.SemaphoreType.DMA((2,)),
                pltpu.SemaphoreType.DMA((2,)),
                pltpu.SemaphoreType.DMA((2, 2 * steps + 1)),
                pltpu.SemaphoreType.REGULAR((2,)),
                pltpu.SemaphoreType.DMA((2,)),
            ],
            compiler_params=pltpu.CompilerParams(
                collective_id=0, has_side_effects=True, vmem_limit_bytes=24 << 20
            ),
        )(*args)
        return pl.pallas_call(
            complete,
            out_shape=[jax.ShapeDtypeStruct((rows, width), jnp.float32)] * 2,
            in_specs=[vmem] * 6,
            out_specs=[hbm] * 2,
            scratch_shapes=[
                pltpu.VMEM((rows, width), jnp.float32),
                pltpu.SemaphoreType.DMA((rows // PART + 1,)),
            ],
            compiler_params=pltpu.CompilerParams(vmem_limit_bytes=24 << 20),
        )(*held)

    rows_spec = P(("blk", "sub"), None)
    return jax.shard_map(
        step, mesh=mesh, in_specs=(rows_spec, rows_spec, P(), P()), out_specs=(rows_spec, rows_spec), check_vma=False
    )
```
